512 devices in a mesh: slab: 32 (over y_lo, x, core), chan: 16 (over y_hi, z).
Axes of the slice: x: 4, y: 8 (y_hi: 2, y_lo: 4; y = y_hi * 4 + y_lo), z: 8, core: 2. Of those that a mesh axis runs over, the one named last changes fastest.
Arguments:
- inputs: bfloat16 [256, 64, 1536], P('chan', 'slab'), may hold values from -6 to 6
- filters: bfloat16 [27, 256, 256], P(None, 'chan'), may hold values from -0.078125 to 0.078125
- cotangent: bfloat16 [256, 64, 1536], P('chan', 'slab'), may hold values from -6 to 6
Outputs:
- features: bfloat16 [256, 64, 1536], P('chan', 'slab')
- input_grad: bfloat16 [256, 64, 1536], P('chan', 'slab')
- filter_grad: float32 [27, 256, 256], P(None, 'chan', 'slab')
The draws below stay inside these ranges and needn't reach their ends.
All inputs are finite; a program needn't handle non-finite values.
Results may differ from the reference program's by a relative error of at most 0.001.
Values may be sent and summed in bfloat16 or wider, within the bound.
No kernel may reach another device: no remote copies, remote signals or barrier semaphores. Data moves between devices by JAX's collectives and lax.ppermute only.
A program may use at most 64 MiB of HBM per device.

```python
import math
import jax
import jax.numpy as jnp

CIN = 256
COUT = 256
H = 24
W = 64
DEPTH = 64
HW = 1536


def with_spikes(entries, own_key, source, target, blocks, factor):
    def block_of(axis_at):
        return (jnp.arange(entries.shape[axis_at]) // (entries.shape[axis_at] // blocks)).reshape((-1,) + (1,) * (entries.ndim - 1 - axis_at))

    one_side = jax.random.permutation(own_key, blocks)[block_of(target)]
    other_side = (block_of(target) + blocks // 2) % blocks
    return jnp.where((block_of(source) == one_side) | (block_of(source) == other_side), factor * entries, entries)


def block_levels(rng, shape, cuts, smallest, high):
    def one(position, blocks):
        steps = jax.random.uniform(jax.random.fold_in(jax.random.fold_in(rng, 6), position), (blocks,), jnp.float32, smallest / len(cuts), high / len(cuts))
        return jnp.repeat(jnp.exp(steps), shape[position] // blocks).reshape((-1,) + (1,) * (len(shape) - position - 1))

    level = one(*cuts[0])
    for cut in cuts[1:]:
        level = level * one(*cut)
    return level


def bell_draw(stream_key, extent, scale, bound, cuts=(), kind=jnp.bfloat16):
    result = scale * jax.random.normal(stream_key, extent, jnp.float32)
    if cuts:
        result = result * block_levels(stream_key, extent, cuts, -0.22, 0.18)
    return jnp.clip(result, -bound, bound).astype(kind)


def gaussian_with(key, dims, deviation, bound, split, heavy, held_as=jnp.bfloat16):
    values = deviation * jax.random.normal(key, dims, jnp.float32)
    if split:
        values = values * block_levels(key, dims, split, -0.22, 0.18)
    return jnp.clip(with_spikes(values, jax.random.fold_in(key, 3), *heavy), -bound, bound).astype(held_as)


def setup_inputs(seed: int = 0) -> dict:
    key_list = jax.random.split(jax.random.key(seed), 4)
    return {
        "inputs": gaussian_with(key_list[0], (CIN, DEPTH, HW), 1.0, 6.0, ((0, 16), (1, 32)), (1, 0, 32, 2.75)),
        "filters": bell_draw(key_list[1], (27, COUT, CIN), (27 * CIN) ** -0.5, 0.078125, ((1, 16),)),
        "cotangent": bell_draw(key_list[2], (COUT, DEPTH, HW), 1.0, 6.0, ((0, 16), (1, 32))),
    }


offsets = (-1, 0, 1)

def reference(inputs, filters, cotangent):
    cells = DEPTH * H * W
    volume = inputs.reshape(CIN, DEPTH, H, W)
    grad_volume = cotangent.reshape(COUT, DEPTH, H, W)
    grad_flat = cotangent.reshape(COUT, cells)
    factor = 1.0 / math.sqrt(cells)
    features = jnp.zeros((COUT, cells), jnp.float32)
    input_grad = jnp.zeros((CIN, cells), jnp.float32)
    blocks = []
    for plane_shift in offsets:
        for row_shift in offsets:
            for column_shift in offsets:
                tap_index = 9 * (plane_shift + 1) + 3 * (row_shift + 1) + column_shift + 1
                shifted = jnp.roll(volume, (-plane_shift, -row_shift, -column_shift), axis=(1, 2, 3)).reshape(CIN, cells)
                unshifted = jnp.roll(grad_volume, (plane_shift, row_shift, column_shift), axis=(1, 2, 3)).reshape(COUT, cells)
                features = features + jnp.dot(filters[tap_index], shifted, preferred_element_type=jnp.float32)
                input_grad = input_grad + jnp.dot(filters[tap_index].T, unshifted, preferred_element_type=jnp.float32)
                blocks.append(jnp.dot(grad_flat, shifted.T, preferred_element_type=jnp.float32) * factor)
    features = features.astype(jnp.bfloat16).reshape(COUT, DEPTH, H * W)
    input_grad = input_grad.astype(jnp.bfloat16).reshape(CIN, DEPTH, H * W)
    return (features, input_grad, jnp.stack(blocks))
```

```python
import functools
import math

import jax
import jax.numpy as jnp
from jax import lax
from jax.experimental import pallas as pl
from jax.experimental.pallas import tpu as pltpu
from jax.sharding import Mesh, PartitionSpec as P

AXES = ("yl1", "yl0", "x", "core", "yh", "z")
SIZES = (2, 2, 4, 2, 2, 8)
W = 64
PLANE = 1536
BF = jnp.bfloat16
F32 = jnp.float32
SLAB = ("yl1", "yl0", "x", "core")
RING = (0, -1, 1, -2, 2, -3, 3, 4)


def shift_pairs(size, step):
    return [(i, (i + step) % size) for i in range(size)]


def shift_add(rows, sign):
    lane = lax.broadcasted_iota(jnp.int32, (16, 128), 1)
    low = lane < 64
    edge_up = (lane % 64) == 63
    edge_down = (lane % 64) == 0
    count = PLANE // 128
    out = [None] * count
    for r in (-1, 0, 1):
        step = sign * r
        total = []
        taps = []
        for q in (-1, 0, 1):
            v = rows(3 * (q + 1) + r + 1)
            taps.append([v[:, 128 * i : 128 * i + 128] for i in range(count)])
        by_step = {sign * q: taps[q + 1] for q in (-1, 0, 1)}
        up = [pltpu.roll(v, 64, 1) for v in by_step[1]]
        down = [pltpu.roll(v, 64, 1) for v in by_step[-1]]
        for i in range(count):
            a = jnp.where(low, up[i], up[(i + 1) % count])
            b = jnp.where(low, down[(i - 1) % count], down[i])
            total.append(by_step[0][i] + a + b)
        for i in range(count):
            v = total[i]
            if step == 1:
                v = jnp.where(edge_up, pltpu.roll(v, 63, 1), pltpu.roll(v, 127, 1))
            elif step == -1:
                v = jnp.where(edge_down, pltpu.roll(v, 65, 1), pltpu.roll(v, 1, 1))
            out[i] = v if out[i] is None else out[i] + v
    return out


def gather_blocks(z_ref, part, blocks, low, high, field):
    z = z_ref[0]
    for j, off in enumerate(RING):
        row = pl.multiple_of(lax.rem(z + off + 8, 8) * 16, 16)
        for d in range(2):
            field[pl.ds((d + 1) * 128 + row, 16), :] = blocks[j](d)
        field[pl.ds(row, 16), :] = low[part, j]
        field[pl.ds(384 + row, 16), :] = high[part, j]


def conv(field, weights, prod, out_own, out_far, sign):
    for d in range(2):
        prod[...] = jnp.dot(
            weights[...], field[pl.ds(d * 128, 384), :], preferred_element_type=F32
        )
        for m, out in enumerate((out_own, out_far)):
            cols = shift_add(lambda k: prod[pl.ds(m * 144 + k * 16, 16), :], sign)
            for i, v in enumerate(cols):
                out[:, pl.ds(d * PLANE + i * 128, 128)] = v


def blocks_of(refs, last, part):
    def at(j):
        if j == 7:
            return lambda d: last[d]
        return lambda d: refs[j][part, d]

    return [at(j) for j in range(8)]


def features_kernel(z_ref, *refs):
    ring, last, low, high, own, far, weights = refs[:7], *refs[7:13]
    out_own, out_far, out_filter, field, prod, shifted = refs[13:]
    gather_blocks(z_ref, 0, blocks_of(ring, last, 0), low, high, field)
    conv(field, weights, prod, out_own, out_far, 1)
    lane = lax.broadcasted_iota(jnp.int32, (16, 128), 1)
    left = lane < 64
    edge_up = (lane % 64) == 63
    edge_down = (lane % 64) == 0
    count = PLANE // 128
    for m in range(2):
        for d in range(2):
            v = (own[1, d] if m == 0 else far[d]).astype(F32)
            base = [v[:, 128 * i : 128 * i + 128] for i in range(count)]
            for r in (-1, 0, 1):
                if r == 0:
                    col = base
                elif r == 1:
                    col = [jnp.where(edge_down, pltpu.roll(a, 65, 1), pltpu.roll(a, 1, 1)) for a in base]
                else:
                    col = [jnp.where(edge_up, pltpu.roll(a, 63, 1), pltpu.roll(a, 127, 1)) for a in base]
                half = [pltpu.roll(a, 64, 1) for a in col]
                for q in (-1, 0, 1):
                    row = m * 144 + (3 * (q + 1) + r + 1) * 16
                    for i in range(count):
                        if q == 0:
                            a = col[i]
                        elif q == 1:
                            a = jnp.where(left, half[(i - 1) % count], half[i])
                        else:
                            a = jnp.where(left, half[i], half[(i + 1) % count])
                        shifted[pl.ds(row, 16), pl.ds(d * PLANE + i * 128, 128)] = a.astype(BF)
    total = None
    for d in range(2):
        part = lax.dot_general(
            field[pl.ds(d * 128, 384), :],
            shifted[:, pl.ds(d * PLANE, PLANE)],
            (((1,), (1,)), ((), ())),
            preferred_element_type=F32,
        )
        total = part if total is None else total + part
    for m in range(2):
        for p in range(3):
            out_filter[m, :, :, pl.ds(p * 144, 144)] = total[
                p * 128 : p * 128 + 128, m * 144 : m * 144 + 144
            ].reshape(16, 8, 144)


def gradient_kernel(z_ref, *refs):
    ring, last, low, high, weights = refs[:7], *refs[7:11]
    out_own, out_far, field, prod = refs[11:]
    gather_blocks(z_ref, 1, blocks_of(ring, last, 1), low, high, field)
    conv(field, weights, prod, out_own, out_far, -1)


VM = pl.BlockSpec(memory_space=pltpu.VMEM)
SM = pl.BlockSpec(memory_space=pltpu.SMEM)


def local(inputs, filters, cotangent):
    z = lax.axis_index("z")
    yh = lax.axis_index("yh")
    swap = [(0, 1), (1, 0)]
    flat = filters.reshape(432, 256)
    near = lax.dynamic_slice(flat, (0, yh * 128), (432, 128))
    away = lax.dynamic_slice(flat, (0, (1 - yh) * 128), (432, 128))
    far_filters = lax.ppermute(away, "yh", swap)

    row = lax.broadcasted_iota(jnp.int32, (256, 256), 0)
    col = lax.broadcasted_iota(jnp.int32, (256, 256), 1)
    zz, m, i = row // 32, (row // 16) % 2, row % 16
    wanted = ((yh + m) % 2) * 128 + zz * 16 + i
    pick = (col == wanted).astype(BF)
    chunks = lax.dot_general(pick, flat, (((1,), (1,)), ((), ())), preferred_element_type=F32)
    chunks = chunks.astype(BF).reshape(8, 32, 432)
    turned = lax.all_to_all(chunks, "z", 0, 0, tiled=True)
    turned = turned.reshape(8, 2, 16, 3, 9, 16)[:, :, :, ::-1]
    grad_weights = turned.transpose(1, 4, 2, 3, 0, 5).reshape(288, 384)

    def stack_taps(f):
        return f.reshape(3, 144, 128).transpose(1, 0, 2).reshape(144, 384)

    weights = jnp.concatenate([stack_taps(near), stack_taps(far_filters)], 0)

    own = jnp.stack([inputs.transpose(1, 0, 2), cotangent.transpose(1, 0, 2)])
    far = lax.ppermute(own[1], "yh", swap)
    up, down = shift_pairs(8, 1), shift_pairs(8, -1)
    blocks = [own]
    a = b = own
    for _ in range(3):
        a = lax.ppermute(a, "z", up)
        b = lax.ppermute(b, "z", down)
        blocks += [a, b]
    last_x = lax.ppermute(a[0], "z", up)
    last_g = lax.ppermute(b[1], "z", down)

    def rim(d):
        parts = [v[:, d] for v in blocks]
        parts.append(jnp.stack([last_x[d], last_g[d]]))
        return jnp.stack(parts, 1)

    low = lax.ppermute(rim(1), SLAB, shift_pairs(32, 1))
    high = lax.ppermute(rim(0), SLAB, shift_pairs(32, -1))

    zs = z.reshape(1).astype(jnp.int32)
    piece = jax.ShapeDtypeStruct((16, 2 * PLANE), F32)
    params = pltpu.CompilerParams(vmem_limit_bytes=48 * 1024 * 1024)
    feat_own, feat_far, filt = pl.pallas_call(
        features_kernel,
        out_shape=(piece, piece, jax.ShapeDtypeStruct((2, 16, 8, 432), F32)),
        in_specs=[SM] + [VM] * 13,
        out_specs=(VM, VM, VM),
        scratch_shapes=[
            pltpu.VMEM((512, PLANE), BF),
            pltpu.VMEM((288, PLANE), F32),
            pltpu.VMEM((288, 2 * PLANE), BF),
        ],
        compiler_params=params,
    )(zs, *blocks, last_x, low, high, own, far, weights)
    grad_own, grad_far = pl.pallas_call(
        gradient_kernel,
        out_shape=(piece, piece),
        in_specs=[SM] + [VM] * 11,
        out_specs=(VM, VM),
        scratch_shapes=[pltpu.VMEM((512, PLANE), BF), pltpu.VMEM((288, PLANE), F32)],
        compiler_params=params,
    )(zs, *blocks, last_g, low, high, grad_weights)

    feat_in = lax.ppermute(feat_far, "yh", swap)
    grad_in = lax.ppermute(grad_far, "yh", swap)
    got = lax.all_to_all(filt.reshape(32, 8, 432), SLAB, 0, 0, tiled=True)
    factor = 1.0 / math.sqrt(64 * PLANE)
    mine = got.sum(0) * factor
    pairs = []
    for yl1 in range(2):
        for h in range(2):
            pairs.append((yl1 * 2 + h, h * 2 + (yl1 ^ h)))
    mine = lax.ppermute(mine, ("yl1", "yh"), pairs)
    filter_grad = mine.reshape(8, 27, 16).transpose(1, 2, 0)
    features = (feat_own + feat_in).astype(BF).reshape(16, 2, PLANE)
    input_grad = (grad_own + grad_in).astype(BF).reshape(16, 2, PLANE)
    return features, input_grad, filter_grad


def solution(mesh):
    fine = Mesh(mesh.devices.reshape(SIZES), AXES)
    chan = ("yh", "z")
    field = P(chan, SLAB, None)
    return jax.shard_map(
        local,
        mesh=fine,
        in_specs=(field, P(None, chan, None), field),
        out_specs=(field, field, P(None, chan, SLAB)),
        check_vma=False,
    )
```

```python
import functools
import math

import jax
import jax.numpy as jnp
from jax import lax
from jax.experimental import pallas as pl
from jax.experimental.pallas import tpu as pltpu
from jax.sharding import Mesh, PartitionSpec as P

AXES = ("yl1", "yl0", "x", "core", "yh", "z")
SIZES = (2, 2, 4, 2, 2, 8)
W = 64
PLANE = 1536
BF = jnp.bfloat16
F32 = jnp.float32
SLAB = ("yl1", "yl0", "x", "core")
RING = (0, -1, 1, -2, 2, -3, 3, 4)


def shift_pairs(size, step):
    return [(i, (i + step) % size) for i in range(size)]


def shift_add(rows, sign):
    lane = lax.broadcasted_iota(jnp.int32, (16, 128), 1)
    low = lane < 64
    edge_up = (lane % 64) == 63
    edge_down = (lane % 64) == 0
    count = PLANE // 128
    out = [None] * count
    for r in (-1, 0, 1):
        step = sign * r
        total = []
        taps = []
        for q in (-1, 0, 1):
            v = rows(3 * (q + 1) + r + 1)
            taps.append([v[:, 128 * i : 128 * i + 128] for i in range(count)])
        by_step = {sign * q: taps[q + 1] for q in (-1, 0, 1)}
        up = [pltpu.roll(v, 64, 1) for v in by_step[1]]
        down = [pltpu.roll(v, 64, 1) for v in by_step[-1]]
        for i in range(count):
            a = jnp.where(low, up[i], up[(i + 1) % count])
            b = jnp.where(low, down[(i - 1) % count], down[i])
            total.append(by_step[0][i] + a + b)
        for i in range(count):
            v = total[i]
            if step == 1:
                v = jnp.where(edge_up, pltpu.roll(v, 63, 1), pltpu.roll(v, 127, 1))
            elif step == -1:
                v = jnp.where(edge_down, pltpu.roll(v, 65, 1), pltpu.roll(v, 1, 1))
            out[i] = v if out[i] is None else out[i] + v
    return out


def gather_blocks(info, part, blocks, inner, outer, field):
    z, core = info[0], info[1]
    inner_at, outer_at = (1 - core) * 384, core * 384
    for j, off in enumerate(RING):
        row = pl.multiple_of(lax.rem(z + off + 8, 8) * 16, 16)
        for d in range(2):
            field[pl.ds((d + 1) * 128 + row, 16), :] = blocks[j](d)
        field[pl.ds(pl.multiple_of(inner_at + row, 16), 16), :] = inner[j, part]
        field[pl.ds(pl.multiple_of(outer_at + row, 16), 16), :] = outer[j, part]


def conv(field, weights, prod, out_own, out_far, sign):
    for d in range(2):
        prod[...] = jnp.dot(
            weights[...], field[pl.ds(d * 128, 384), :], preferred_element_type=F32
        )
        for m, out in enumerate((out_own, out_far)):
            cols = shift_add(lambda k: prod[pl.ds(m * 144 + k * 16, 16), :], sign)
            for i, v in enumerate(cols):
                out[:, pl.ds(d * PLANE + i * 128, 128)] = v


def blocks_of(refs, last, part):
    def at(j):
        if j == 7:
            return lambda d: last[d]
        return lambda d: refs[j][d, part]

    return [at(j) for j in range(8)]


def grad_weights(turned, weights):
    lane = lax.broadcasted_iota(jnp.int32, (32, 128), 1) // 16
    got = [turned[k].astype(F32) for k in range(8)]
    for t in range(27):
        p, qr = t // 9, t % 9
        lo = t * 16 // 128 * 128
        total = None
        for k in range(8):
            v = got[k][:, lo : lo + 128]
            v = pltpu.roll(v, (16 * k - (t * 16 - lo)) % 128, 1)
            total = v if total is None else jnp.where(lane == k, v, total)
        total = total.astype(BF)
        for m in range(2):
            weights[pl.ds(m * 144 + qr * 16, 16), pl.ds((2 - p) * 128, 128)] = total[
                16 * m : 16 * m + 16
            ]


def rims_kernel(info, *refs):
    ring, last_x, last_g = refs[:7], *refs[7:9]
    inner, outer = refs[9:]
    core = info[1]
    for j in range(7):
        inner[j] = ring[j][1 - core]
        outer[j] = ring[j][core]
    inner[7, 0] = last_x[1 - core]
    inner[7, 1] = last_g[1 - core]
    outer[7, 0] = last_x[core]
    outer[7, 1] = last_g[core]


def features_kernel(info, *refs):
    ring, last, inner, outer, near, away = refs[:7], *refs[7:12]
    out_own, out_far, field, prod, weights = refs[12:]
    gather_blocks(info, 0, blocks_of(ring, last, 0), inner, outer, field)
    for m, f in enumerate((near, away)):
        for p in range(3):
            weights[pl.ds(m * 144, 144), pl.ds(p * 128, 128)] = f[pl.ds(p * 144, 144), :]
    conv(field, weights, prod, out_own, out_far, 1)


def filter_kernel(info, *refs):
    ring, last, inner, outer, far, _after = refs[:7], *refs[7:12]
    out_filter, field, shifted = refs[12:]
    gather_blocks(info, 0, blocks_of(ring, last, 0), inner, outer, field)
    filter_part(ring[0], far, field, shifted, out_filter)


def gradient_kernel(info, *refs):
    ring, last, inner, outer, turned, _after = refs[:7], *refs[7:12]
    out_own, out_far, field, prod, weights = refs[12:]
    gather_blocks(info, 1, blocks_of(ring, last, 1), inner, outer, field)
    grad_weights(turned, weights)
    conv(field, weights, prod, out_own, out_far, -1)


def chunks_kernel(pick, flat, _after, out):
    v = lax.dot_general(
        pick[...], flat[...], (((1,), (1,)), ((), ())), preferred_element_type=F32
    ).astype(BF)
    for k in range(8):
        out[k, :, pl.ds(0, 432)] = v[32 * k : 32 * k + 32]
        out[k, :, pl.ds(432, 80)] = jnp.zeros((32, 80), BF)


def filter_part(own, far, x_field, shifted, out_filter):
    lane = lax.broadcasted_iota(jnp.int32, (16, 128), 1)
    left = lane < 64
    edge_up = (lane % 64) == 63
    edge_down = (lane % 64) == 0
    count = PLANE // 128
    for m in range(2):
        for d in range(2):
            v = (own[d, 1] if m == 0 else far[d]).astype(F32)
            base = [v[:, 128 * i : 128 * i + 128] for i in range(count)]
            for r in (-1, 0, 1):
                if r == 0:
                    col = base
                elif r == 1:
                    col = [jnp.where(edge_down, pltpu.roll(a, 65, 1), pltpu.roll(a, 1, 1)) for a in base]
                else:
                    col = [jnp.where(edge_up, pltpu.roll(a, 63, 1), pltpu.roll(a, 127, 1)) for a in base]
                half = [pltpu.roll(a, 64, 1) for a in col]
                for q in (-1, 0, 1):
                    row = m * 144 + (3 * (q + 1) + r + 1) * 16
                    for i in range(count):
                        if q == 0:
                            a = col[i]
                        elif q == 1:
                            a = jnp.where(left, half[(i - 1) % count], half[i])
                        else:
                            a = jnp.where(left, half[i], half[(i + 1) % count])
                        shifted[pl.ds(row, 16), pl.ds(d * PLANE + i * 128, 128)] = a.astype(BF)
    total = None
    for d in range(2):
        part = lax.dot_general(
            x_field[pl.ds(d * 128, 384), :],
            shifted[:, pl.ds(d * PLANE, PLANE)],
            (((1,), (1,)), ((), ())),
            preferred_element_type=F32,
        )
        total = part if total is None else total + part
    for m in range(2):
        for p in range(3):
            out_filter[m, :, :, pl.ds(p * 144, 144)] = total[
                p * 128 : p * 128 + 128, m * 144 : m * 144 + 144
            ].reshape(16, 8, 144)


VM = pl.BlockSpec(memory_space=pltpu.VMEM)
SM = pl.BlockSpec(memory_space=pltpu.SMEM)
ANY = pl.BlockSpec(memory_space=pl.ANY)


def local(inputs, filters, cotangent):
    z = lax.axis_index("z")
    yh = lax.axis_index("yh")
    swap = [(0, 1), (1, 0)]
    flat = filters.reshape(432, 256)
    near = lax.dynamic_slice(flat, (0, yh * 128), (432, 128))
    away = lax.dynamic_slice(flat, (0, (1 - yh) * 128), (432, 128))
    far_filters = lax.ppermute(away, "yh", swap)

    row = lax.broadcasted_iota(jnp.int32, (256, 256), 0)
    col = lax.broadcasted_iota(jnp.int32, (256, 256), 1)
    zz, m, i = row // 32, (row // 16) % 2, row % 16
    wanted = ((yh + m) % 2) * 128 + zz * 16 + i
    pick = (col == wanted).astype(BF)
    own = jnp.stack([inputs, cotangent]).transpose(2, 0, 1, 3)
    far = lax.ppermute(own[:, 1], "yh", swap)
    up, down = shift_pairs(8, 1), shift_pairs(8, -1)
    blocks = [own]
    a = b = own
    for _ in range(3):
        a = lax.ppermute(a, "z", up)
        b = lax.ppermute(b, "z", down)
        blocks += [a, b]
    last_x = lax.ppermute(a[:, 0], "z", up)
    last_g = lax.ppermute(b[:, 1], "z", down)
    core = lax.axis_index("core")
    info = jnp.stack([z, core]).astype(jnp.int32)

    def call(body, outs, in_specs, scratch=()):
        return pl.pallas_call(
            body,
            out_shape=outs,
            in_specs=in_specs,
            out_specs=jax.tree.map(lambda _: VM, outs),
            scratch_shapes=scratch,
            compiler_params=pltpu.CompilerParams(vmem_limit_bytes=48 * 1024 * 1024),
        )

    shape = jax.ShapeDtypeStruct
    rim = shape((8, 2, 16, PLANE), BF)
    inner, outer = call(rims_kernel, (rim, rim), [SM] + [VM] * 9)(info, *blocks, last_x, last_g)
    outer = lax.ppermute(outer, SLAB, [(s, (s + (1 if s % 2 else -1)) % 32) for s in range(32)])
    inner = lax.ppermute(inner, "core", swap)
    chunks = call(chunks_kernel, shape((8, 32, 512), BF), [VM, VM, ANY])(pick, flat, inner)
    turned = lax.all_to_all(chunks, "z", 0, 0, tiled=True)

    piece = shape((16, 2 * PLANE), F32)
    field = pltpu.VMEM((512, PLANE), BF)
    prod = pltpu.VMEM((288, PLANE), F32)
    weights = pltpu.VMEM((288, 384), BF)
    feat_own, feat_far = call(
        features_kernel, (piece, piece), [SM] + [VM] * 12, [field, prod, weights]
    )(info, *blocks, last_x, inner, outer, near, far_filters)
    feat_in = lax.ppermute(feat_far, "yh", swap)
    filt = call(
        filter_kernel,
        shape((2, 16, 8, 432), F32),
        [SM] + [VM] * 11 + [ANY],
        [field, pltpu.VMEM((288, 2 * PLANE), BF)],
    )(info, *blocks, last_x, inner, outer, far, feat_far)
    got = lax.all_to_all(filt.reshape(32, 8, 432), SLAB, 0, 0, tiled=True)
    grad_own, grad_far = call(
        gradient_kernel, (piece, piece), [SM] + [VM] * 11 + [ANY], [field, prod, weights]
    )(info, *blocks, last_g, inner, outer, turned, filt)
    grad_in = lax.ppermute(grad_far, "yh", swap)
    factor = 1.0 / math.sqrt(64 * PLANE)
    mine = got.sum(0) * factor
    pairs = []
    for yl1 in range(2):
        for h in range(2):
            pairs.append((yl1 * 2 + h, h * 2 + (yl1 ^ h)))
    mine = lax.ppermute(mine, ("yl1", "yh"), pairs)
    filter_grad = mine.reshape(8, 27, 16).transpose(1, 2, 0)
    features = (feat_own + feat_in).astype(BF).reshape(16, 2, PLANE)
    input_grad = (grad_own + grad_in).astype(BF).reshape(16, 2, PLANE)
    return features, input_grad, filter_grad


def solution(mesh):
    fine = Mesh(mesh.devices.reshape(SIZES), AXES)
    chan = ("yh", "z")
    field = P(chan, SLAB, None)
    return jax.shard_map(
        local,
        mesh=fine,
        in_specs=(field, P(None, chan, None), field),
        out_specs=(field, field, P(None, chan, SLAB)),
        check_vma=False,
    )
```

```python
import math

import jax
import jax.numpy as jnp
from jax import lax
from jax.experimental import pallas as pl
from jax.experimental.pallas import tpu as pltpu
from jax.sharding import Mesh, PartitionSpec as P


AXES = ("yl1", "yl0", "x", "core", "yh", "z")
SIZES = (2, 2, 4, 2, 2, 8)
PLANE = 1536
BF = jnp.bfloat16
F32 = jnp.float32
SLAB = ("yl1", "yl0", "x", "core")
RING = (0, -1, 1, -2, 2, -3, 3, 4)


def shift_pairs(size, step):
    return [(i, (i + step) % size) for i in range(size)]


def shift_add(rows, sign):
    lane = lax.broadcasted_iota(jnp.int32, (16, 128), 1)
    low = lane < 64
    edge_up = (lane % 64) == 63
    edge_down = (lane % 64) == 0
    count = PLANE // 128
    out = [None] * count
    for r in (-1, 0, 1):
        step = sign * r
        total = []
        taps = []
        for q in (-1, 0, 1):
            v = rows(3 * (q + 1) + r + 1)
            taps.append([v[:, 128 * i : 128 * i + 128] for i in range(count)])
        by_step = {sign * q: taps[q + 1] for q in (-1, 0, 1)}
        up = [pltpu.roll(v, 64, 1) for v in by_step[1]]
        down = [pltpu.roll(v, 64, 1) for v in by_step[-1]]
        for i in range(count):
            a = jnp.where(low, up[i], up[(i + 1) % count])
            b = jnp.where(low, down[(i - 1) % count], down[i])
            total.append(by_step[0][i] + a + b)
        for i in range(count):
            v = total[i]
            if step == 1:
                v = jnp.where(edge_up, pltpu.roll(v, 63, 1), pltpu.roll(v, 127, 1))
            elif step == -1:
                v = jnp.where(edge_down, pltpu.roll(v, 65, 1), pltpu.roll(v, 1, 1))
            out[i] = v if out[i] is None else out[i] + v
    return out


def gather_blocks(info, part, blocks, inner, outer, field):
    z, core = info[0], info[1]
    inner_at, outer_at = (1 - core) * 384, core * 384
    for j, off in enumerate(RING):
        row = pl.multiple_of(lax.rem(z + off + 8, 8) * 16, 16)
        for d in range(2):
            field[pl.ds((d + 1) * 128 + row, 16), :] = blocks[j][d, part]
        field[pl.ds(pl.multiple_of(inner_at + row, 16), 16), :] = inner[j, part]
        field[pl.ds(pl.multiple_of(outer_at + row, 16), 16), :] = outer[j]


def conv(field, weights, prod, out_own, out_far, sign):
    for d in range(2):
        prod[...] = jnp.dot(
            weights[...], field[pl.ds(d * 128, 384), :], preferred_element_type=F32
        )
        for m, out in enumerate((out_own, out_far)):
            cols = shift_add(lambda k: prod[pl.ds(m * 144 + k * 16, 16), :], sign)
            for i, v in enumerate(cols):
                out[:, pl.ds(d * PLANE + i * 128, 128)] = v


def grad_weights(turned, weights):
    lane = lax.broadcasted_iota(jnp.int32, (32, 128), 1) // 16
    got = [turned[k].astype(F32) for k in range(8)]
    for t in range(27):
        p, qr = t // 9, t % 9
        lo = t * 16 // 128 * 128
        total = None
        for k in range(8):
            v = got[k][:, lo : lo + 128]
            v = pltpu.roll(v, (16 * k - (t * 16 - lo)) % 128, 1)
            total = v if total is None else jnp.where(lane == k, v, total)
        total = total.astype(BF)
        for m in range(2):
            weights[pl.ds(m * 144 + qr * 16, 16), pl.ds((2 - p) * 128, 128)] = total[
                16 * m : 16 * m + 16
            ]


def rims_kernel(info, *refs):
    ring, (inner, outer_x, outer_g) = refs[:8], refs[8:]
    core = info[1]
    for j in range(8):
        inner[j] = ring[j][1 - core]
        outer_x[j] = ring[j][core, 0]
        outer_g[j] = ring[j][core, 1]


def fold_kernel(info, got, out):
    yh = info[2]
    sums = []
    for k in range(4):
        v = got[0, k]
        for i in range(1, 8):
            v = v + got[i, k]
        sums.append(v)
    for a in range(2):
        for b in range(2):
            for h in range(2):
                v = jnp.where(yh == 0, sums[h * 2 + b], sums[(1 - h) * 2 + b])
                out[(a * 2 + b) * 2 + h] = jnp.where(yh == a, v, jnp.zeros_like(v))


def pack_kernel(info, own, flat, *refs):
    out = refs[-1]
    out[pl.ds(0, 432), :] = flat[:, pl.ds(pl.multiple_of((1 - info[2]) * 128, 128), 128)]
    for d in range(2):
        for i in range(PLANE // 128):
            out[pl.ds(432 + (d * 12 + i) * 16, 16), :] = own[d, 1, :, pl.ds(i * 128, 128)]


def features_kernel(info, *refs):
    ring, (inner, outer, flat, packed) = refs[:8], refs[8:12]
    out_own, out_far, field, prod, weights = refs[12:]
    gather_blocks(info, 0, ring, inner, outer, field)
    half = pl.ds(pl.multiple_of(info[2] * 128, 128), 128)
    for p in range(3):
        rows, cols = pl.ds(p * 144, 144), pl.ds(p * 128, 128)
        weights[pl.ds(0, 144), cols] = flat[rows, half]
        weights[pl.ds(144, 144), cols] = packed[rows, :]
    conv(field, weights, prod, out_own, out_far, 1)


def filter_kernel(info, *refs):
    ring, (inner, outer, packed) = refs[:8], refs[8:11]
    out_filter, field, shifted = refs[11:]
    gather_blocks(info, 0, ring, inner, outer, field)
    filter_part(ring[0], packed, field, shifted, out_filter)


def gradient_kernel(info, *refs):
    ring, (inner, outer, turned) = refs[:8], refs[8:11]
    out_own, out_far, field, prod, weights = refs[11:]
    gather_blocks(info, 1, ring, inner, outer, field)
    grad_weights(turned, weights)
    conv(field, weights, prod, out_own, out_far, -1)


def chunks_kernel(pick, flat, out):
    v = lax.dot_general(
        pick[...], flat[...], (((1,), (1,)), ((), ())), preferred_element_type=F32
    ).astype(BF)
    for k in range(8):
        out[k, :, pl.ds(0, 432)] = v[32 * k : 32 * k + 32]
        out[k, :, pl.ds(432, 80)] = jnp.zeros((32, 80), BF)


def filter_part(own, packed, x_field, shifted, out_filter):
    lane = lax.broadcasted_iota(jnp.int32, (16, 128), 1)
    left = lane < 64
    edge_up = (lane % 64) == 63
    edge_down = (lane % 64) == 0
    count = PLANE // 128
    for m in range(2):
        for d in range(2):
            if m == 0:
                base = [own[d, 1, :, pl.ds(128 * i, 128)] for i in range(count)]
            else:
                base = [packed[pl.ds(432 + (d * 12 + i) * 16, 16), :] for i in range(count)]
            base = [v.astype(F32) for v in base]
            for r in (-1, 0, 1):
                if r == 0:
                    col = base
                elif r == 1:
                    col = [jnp.where(edge_down, pltpu.roll(a, 65, 1), pltpu.roll(a, 1, 1)) for a in base]
                else:
                    col = [jnp.where(edge_up, pltpu.roll(a, 63, 1), pltpu.roll(a, 127, 1)) for a in base]
                half = [pltpu.roll(a, 64, 1) for a in col]
                for q in (-1, 0, 1):
                    row = m * 144 + (3 * (q + 1) + r + 1) * 16
                    for i in range(count):
                        if q == 0:
                            a = col[i]
                        elif q == 1:
                            a = jnp.where(left, half[(i - 1) % count], half[i])
                        else:
                            a = jnp.where(left, half[i], half[(i + 1) % count])
                        shifted[pl.ds(row, 16), pl.ds(d * PLANE + i * 128, 128)] = a.astype(BF)
    total = None
    for d in range(2):
        part = lax.dot_general(
            x_field[pl.ds(d * 128, 384), :],
            shifted[:, pl.ds(d * PLANE, PLANE)],
            (((1,), (1,)), ((), ())),
            preferred_element_type=F32,
        )
        total = part if total is None else total + part
    for m in range(2):
        for yl0 in range(2):
            for p in range(3):
                row = p * 128 + yl0 * 64
                out_filter[:, m * 2 + yl0, :, pl.ds(p * 144, 144)] = total[
                    row : row + 64, m * 144 : m * 144 + 144
                ].reshape(8, 8, 144)


VM = pl.BlockSpec(memory_space=pltpu.VMEM)
SM = pl.BlockSpec(memory_space=pltpu.SMEM)


def call(body, outs, in_specs, scratch=()):
    return pl.pallas_call(
        body,
        out_shape=outs,
        in_specs=in_specs,
        out_specs=jax.tree.map(lambda _: VM, outs),
        scratch_shapes=scratch,
        compiler_params=pltpu.CompilerParams(vmem_limit_bytes=48 * 1024 * 1024),
    )


def run(inputs, filters, cotangent):
    z, yh, core = lax.axis_index("z"), lax.axis_index("yh"), lax.axis_index("core")
    info = jnp.stack([z, core, yh]).astype(jnp.int32)
    shape = jax.ShapeDtypeStruct
    swap = [(0, 1), (1, 0)]
    flat = filters.reshape(432, 256)

    own = jnp.stack([inputs, cotangent]).transpose(2, 0, 1, 3)
    up, down = shift_pairs(8, 1), shift_pairs(8, -1)
    blocks = [own]
    a = b = own
    for _ in range(3):
        a = lax.ppermute(a, "z", up)
        b = lax.ppermute(b, "z", down)
        blocks += [a, b]
    blocks.append(lax.ppermute(own, "z", shift_pairs(8, 4)))

    packed = call(pack_kernel, shape((816, 128), BF), [SM, VM, VM])(info, own, flat)
    packed = lax.ppermute(packed, "yh", swap)

    rim = shape((8, 2, 16, PLANE), BF)
    half = shape((8, 16, PLANE), BF)
    inner, outer_x, outer_g = call(rims_kernel, (rim, half, half), [SM] + [VM] * 8)(info, *blocks)
    outer_pairs = [(s, (s + (1 if s % 2 else -1)) % 32) for s in range(32)]
    outer_x = lax.ppermute(outer_x, SLAB, outer_pairs)
    outer_g = lax.ppermute(outer_g, SLAB, outer_pairs)
    inner = lax.ppermute(inner, "core", swap)

    row = lax.broadcasted_iota(jnp.int32, (256, 256), 0)
    col = lax.broadcasted_iota(jnp.int32, (256, 256), 1)
    zz, m, i = row // 32, (row // 16) % 2, row % 16
    wanted = ((yh + m) % 2) * 128 + zz * 16 + i
    pick = (col == wanted).astype(BF)
    chunks = call(chunks_kernel, shape((8, 32, 512), BF), [VM, VM])(pick, flat)
    turned = lax.all_to_all(chunks, "z", 0, 0, tiled=True)

    piece = shape((16, 2 * PLANE), F32)
    field = pltpu.VMEM((512, PLANE), BF)
    prod = pltpu.VMEM((288, PLANE), F32)
    weights = pltpu.VMEM((288, 384), BF)
    filt = call(
        filter_kernel,
        shape((8, 4, 8, 432), F32),
        [SM] + [VM] * 11,
        [field, pltpu.VMEM((288, 2 * PLANE), BF)],
    )(info, *blocks, inner, outer_x, packed)
    got = lax.all_to_all(filt, ("x", "core"), 0, 0, tiled=True)
    feat_own, feat_far = call(
        features_kernel, (piece, piece), [SM] + [VM] * 12, [field, prod, weights]
    )(info, *blocks, inner, outer_x, flat, packed)
    feat_in = lax.ppermute(feat_far, "yh", swap)
    grad_own, grad_far = call(
        gradient_kernel, (piece, piece), [SM] + [VM] * 11, [field, prod, weights]
    )(info, *blocks, inner, outer_g, turned)
    grad_in = lax.ppermute(grad_far, "yh", swap)

    got = call(fold_kernel, shape((8, 8, 432), F32), [SM, VM])(info, got)
    got = lax.all_to_all(got, ("yl1", "yl0", "yh"), 0, 0, tiled=True)
    mine = got.sum(0) * (1.0 / math.sqrt(64 * PLANE))
    filter_grad = mine.reshape(8, 27, 16).transpose(1, 2, 0)
    features = (feat_own + feat_in).astype(BF).reshape(16, 2, PLANE)
    input_grad = (grad_own + grad_in).astype(BF).reshape(16, 2, PLANE)
    return features, input_grad, filter_grad


def solution(mesh):
    fine = Mesh(mesh.devices.reshape(SIZES), AXES)
    chan = ("yh", "z")
    field = P(chan, SLAB, None)
    return jax.shard_map(
        run,
        mesh=fine,
        in_specs=(field, P(None, chan, None), field),
        out_specs=(field, field, P(None, chan, SLAB)),
        check_vma=False,
    )
```

```python
import math

import jax
import jax.numpy as jnp
from jax import lax
from jax.experimental import pallas as pl
from jax.experimental.pallas import tpu as pltpu
from jax.sharding import Mesh, PartitionSpec as P


AXES = ("yl1", "yl0", "x", "core", "yh", "z")
SIZES = (2, 2, 4, 2, 2, 8)
PLANE = 1536
BF = jnp.bfloat16
F32 = jnp.float32
SLAB = ("yl1", "yl0", "x", "core")
RING = (0, -1, 1, -2, 2, -3, 3, 4)


def shift_pairs(size, step):
    return [(i, (i + step) % size) for i in range(size)]


def shift_add(rows, sign):
    lane = lax.broadcasted_iota(jnp.int32, (16, 128), 1)
    low = lane < 64
    edge_up = (lane % 64) == 63
    edge_down = (lane % 64) == 0
    count = PLANE // 128
    out = [None] * count
    for r in (-1, 0, 1):
        step = sign * r
        total = []
        taps = []
        for q in (-1, 0, 1):
            v = rows(3 * (q + 1) + r + 1)
            taps.append([v[:, 128 * i : 128 * i + 128] for i in range(count)])
        by_step = {sign * q: taps[q + 1] for q in (-1, 0, 1)}
        up = [pltpu.roll(v, 64, 1) for v in by_step[1]]
        down = [pltpu.roll(v, 64, 1) for v in by_step[-1]]
        for i in range(count):
            a = jnp.where(low, up[i], up[(i + 1) % count])
            b = jnp.where(low, down[(i - 1) % count], down[i])
            total.append(by_step[0][i] + a + b)
        for i in range(count):
            v = total[i]
            if step == 1:
                v = jnp.where(edge_up, pltpu.roll(v, 63, 1), pltpu.roll(v, 127, 1))
            elif step == -1:
                v = jnp.where(edge_down, pltpu.roll(v, 65, 1), pltpu.roll(v, 1, 1))
            out[i] = v if out[i] is None else out[i] + v
    return out


def gather_blocks(info, part, blocks, inner, outer, field):
    z, core = info[0], info[1]
    inner_at, outer_at = (1 - core) * 384, core * 384
    for j, off in enumerate(RING):
        row = pl.multiple_of(lax.rem(z + off + 8, 8) * 16, 16)
        for d in range(2):
            field[pl.ds((d + 1) * 128 + row, 16), :] = blocks[j][d, part]
        field[pl.ds(pl.multiple_of(inner_at + row, 16), 16), :] = inner[j, part]
        field[pl.ds(pl.multiple_of(outer_at + row, 16), 16), :] = outer[j]


def conv(field, weights, prod, out_own, out_far, sign):
    for d in range(2):
        prod[...] = jnp.dot(
            weights[...], field[pl.ds(d * 128, 384), :], preferred_element_type=F32
        )
        for m, out in enumerate((out_own, out_far)):
            cols = shift_add(lambda k: prod[pl.ds(m * 144 + k * 16, 16), :], sign)
            for i, v in enumerate(cols):
                out[:, pl.ds(d * PLANE + i * 128, 128)] = v


def grad_weights(turned, weights):
    lane = lax.broadcasted_iota(jnp.int32, (32, 128), 1) // 16
    got = [turned[k].astype(F32) for k in range(8)]
    for t in range(27):
        p, qr = t // 9, t % 9
        lo = t * 16 // 128 * 128
        total = None
        for k in range(8):
            v = got[k][:, lo : lo + 128]
            v = pltpu.roll(v, (16 * k - (t * 16 - lo)) % 128, 1)
            total = v if total is None else jnp.where(lane == k, v, total)
        total = total.astype(BF)
        for m in range(2):
            weights[pl.ds(m * 144 + qr * 16, 16), pl.ds((2 - p) * 128, 128)] = total[
                16 * m : 16 * m + 16
            ]


def rims_kernel(info, *refs):
    ring, (inner, outer_x, outer_g) = refs[:8], refs[8:]
    core = info[1]
    for j in range(8):
        inner[j] = ring[j][1 - core]
        outer_x[j] = ring[j][core, 0]
        outer_g[j] = ring[j][core, 1]


def fold_kernel(info, got, out):
    yh = info[2]
    sums = []
    for k in range(4):
        v = got[0, k]
        for i in range(1, 8):
            v = v + got[i, k]
        sums.append(v)
    for a in range(2):
        for b in range(2):
            for h in range(2):
                v = jnp.where(yh == 0, sums[h * 2 + b], sums[(1 - h) * 2 + b])
                out[(a * 2 + b) * 2 + h] = jnp.where(yh == a, v, jnp.zeros_like(v))


def pack_kernel(info, own, flat, *refs):
    out = refs[-1]
    out[pl.ds(0, 432), :] = flat[:, pl.ds(pl.multiple_of((1 - info[2]) * 128, 128), 128)]
    for d in range(2):
        for i in range(PLANE // 128):
            out[pl.ds(432 + (d * 12 + i) * 16, 16), :] = own[d, 1, :, pl.ds(i * 128, 128)]


def features_kernel(info, *refs):
    ring, (inner, outer, flat, packed) = refs[:8], refs[8:12]
    out_own, out_far, field, prod, weights = refs[12:]
    gather_blocks(info, 0, ring, inner, outer, field)
    half = pl.ds(pl.multiple_of(info[2] * 128, 128), 128)
    for p in range(3):
        rows, cols = pl.ds(p * 144, 144), pl.ds(p * 128, 128)
        weights[pl.ds(0, 144), cols] = flat[rows, half]
        weights[pl.ds(144, 144), cols] = packed[rows, :]
    conv(field, weights, prod, out_own, out_far, 1)


def filter_kernel(info, *refs):
    ring, (inner, outer, packed) = refs[:8], refs[8:11]
    out_filter, field, shifted = refs[11:]
    gather_blocks(info, 0, ring, inner, outer, field)
    filter_part(ring[0], packed, field, shifted, out_filter)


def gradient_kernel(info, *refs):
    ring, (inner, outer, turned) = refs[:8], refs[8:11]
    out_own, out_far, field, prod, weights = refs[11:]
    gather_blocks(info, 1, ring, inner, outer, field)
    grad_weights(turned, weights)
    conv(field, weights, prod, out_own, out_far, -1)


def chunks_kernel(info, flat, out):
    row = lax.broadcasted_iota(jnp.int32, (256, 256), 0)
    col = lax.broadcasted_iota(jnp.int32, (256, 256), 1)
    half = (info[2] + (row >> 4)) & 1
    pick = (col == half * 128 + (row >> 5) * 16 + (row & 15)).astype(F32).astype(BF)
    v = lax.dot_general(
        pick, flat[...], (((1,), (1,)), ((), ())), preferred_element_type=F32
    ).astype(BF)
    for k in range(8):
        out[k, :, pl.ds(0, 432)] = v[32 * k : 32 * k + 32]
        out[k, :, pl.ds(432, 80)] = jnp.zeros((32, 80), BF)


def filter_part(own, packed, x_field, shifted, out_filter):
    lane = lax.broadcasted_iota(jnp.int32, (16, 128), 1)
    left = lane < 64
    edge_up = (lane % 64) == 63
    edge_down = (lane % 64) == 0
    count = PLANE // 128
    for m in range(2):
        for d in range(2):
            if m == 0:
                base = [own[d, 1, :, pl.ds(128 * i, 128)] for i in range(count)]
            else:
                base = [packed[pl.ds(432 + (d * 12 + i) * 16, 16), :] for i in range(count)]
            base = [v.astype(F32) for v in base]
            for r in (-1, 0, 1):
                if r == 0:
                    col = base
                elif r == 1:
                    col = [jnp.where(edge_down, pltpu.roll(a, 65, 1), pltpu.roll(a, 1, 1)) for a in base]
                else:
                    col = [jnp.where(edge_up, pltpu.roll(a, 63, 1), pltpu.roll(a, 127, 1)) for a in base]
                half = [pltpu.roll(a, 64, 1) for a in col]
                for q in (-1, 0, 1):
                    row = m * 144 + (3 * (q + 1) + r + 1) * 16
                    for i in range(count):
                        if q == 0:
                            a = col[i]
                        elif q == 1:
                            a = jnp.where(left, half[(i - 1) % count], half[i])
                        else:
                            a = jnp.where(left, half[i], half[(i + 1) % count])
                        shifted[pl.ds(row, 16), pl.ds(d * PLANE + i * 128, 128)] = a.astype(BF)
    total = None
    for d in range(2):
        part = lax.dot_general(
            x_field[pl.ds(d * 128, 384), :],
            shifted[:, pl.ds(d * PLANE, PLANE)],
            (((1,), (1,)), ((), ())),
            preferred_element_type=F32,
        )
        total = part if total is None else total + part
    for m in range(2):
        for yl0 in range(2):
            for p in range(3):
                row = p * 128 + yl0 * 64
                out_filter[:, m * 2 + yl0, :, pl.ds(p * 144, 144)] = total[
                    row : row + 64, m * 144 : m * 144 + 144
                ].reshape(8, 8, 144)


VM = pl.BlockSpec(memory_space=pltpu.VMEM)
SM = pl.BlockSpec(memory_space=pltpu.SMEM)


def call(body, outs, in_specs, scratch=()):
    return pl.pallas_call(
        body,
        out_shape=outs,
        in_specs=in_specs,
        out_specs=jax.tree.map(lambda _: VM, outs),
        scratch_shapes=scratch,
        compiler_params=pltpu.CompilerParams(vmem_limit_bytes=24 * 1024 * 1024),
    )


def run(inputs, filters, cotangent):
    z, yh, core = lax.axis_index("z"), lax.axis_index("yh"), lax.axis_index("core")
    info = jnp.stack([z, core, yh]).astype(jnp.int32)
    shape = jax.ShapeDtypeStruct
    swap = [(0, 1), (1, 0)]
    flat = filters.reshape(432, 256)

    own = jnp.stack([inputs, cotangent]).transpose(2, 0, 1, 3)
    up, down = shift_pairs(8, 1), shift_pairs(8, -1)
    blocks = [own]
    a = b = own
    for _ in range(3):
        a = lax.ppermute(a, "z", up)
        b = lax.ppermute(b, "z", down)
        blocks += [a, b]
    blocks.append(lax.ppermute(own, "z", shift_pairs(8, 4)))

    packed = call(pack_kernel, shape((816, 128), BF), [SM, VM, VM])(info, own, flat)
    packed = lax.ppermute(packed, "yh", swap)

    rim = shape((8, 2, 16, PLANE), BF)
    half = shape((8, 16, PLANE), BF)
    inner, outer_x, outer_g = call(rims_kernel, (rim, half, half), [SM] + [VM] * 8)(info, *blocks)
    outer_pairs = [(s, (s + (1 if s % 2 else -1)) % 32) for s in range(32)]
    outer_x = lax.ppermute(outer_x, SLAB, outer_pairs)
    outer_g = lax.ppermute(outer_g, SLAB, outer_pairs)
    inner = lax.ppermute(inner, "core", swap)

    chunks = call(chunks_kernel, shape((8, 32, 512), BF), [SM, VM])(info, flat)
    turned = lax.all_to_all(chunks, "z", 0, 0, tiled=True)

    piece = shape((16, 2 * PLANE), F32)
    field = pltpu.VMEM((512, PLANE), BF)
    prod = pltpu.VMEM((288, PLANE), F32)
    weights = pltpu.VMEM((288, 384), BF)
    filt = call(
        filter_kernel,
        shape((8, 4, 8, 432), F32),
        [SM] + [VM] * 11,
        [field, pltpu.VMEM((288, 2 * PLANE), BF)],
    )(info, *blocks, inner, outer_x, packed)
    got = lax.all_to_all(filt, ("x", "core"), 0, 0, tiled=True)
    feat_own, feat_far = call(
        features_kernel, (piece, piece), [SM] + [VM] * 12, [field, prod, weights]
    )(info, *blocks, inner, outer_x, flat, packed)
    feat_in = lax.ppermute(feat_far, "yh", swap)
    grad_own, grad_far = call(
        gradient_kernel, (piece, piece), [SM] + [VM] * 11, [field, prod, weights]
    )(info, *blocks, inner, outer_g, turned)
    grad_in = lax.ppermute(grad_far, "yh", swap)

    got = call(fold_kernel, shape((8, 8, 432), F32), [SM, VM])(info, got)
    got = lax.all_to_all(got, ("yl1", "yl0", "yh"), 0, 0, tiled=True)
    mine = got.sum(0) * (1.0 / math.sqrt(64 * PLANE))
    filter_grad = mine.reshape(8, 27, 16).transpose(1, 2, 0)
    features = (feat_own + feat_in).astype(BF).reshape(16, 2, PLANE)
    input_grad = (grad_own + grad_in).astype(BF).reshape(16, 2, PLANE)
    return features, input_grad, filter_grad


def solution(mesh):
    fine = Mesh(mesh.devices.reshape(SIZES), AXES)
    chan = ("yh", "z")
    field = P(chan, SLAB, None)
    return jax.shard_map(
        run,
        mesh=fine,
        in_specs=(field, P(None, chan, None), field),
        out_specs=(field, field, P(None, chan, SLAB)),
        check_vma=False,
    )
```
